256 devices in a mesh: tm: 8 (over x_lo, y), space: 32 (over x_hi, z, core).
Axes of the slice: x: 4 (x_hi: 2, x_lo: 2; x = x_hi * 2 + x_lo), y: 4, z: 8, core: 2. Of those that a mesh axis runs over, the one named last changes fastest.
Arguments:
- initial_state: float32 [64, 256, 256], P('space'), may hold values from -6 to 6
- capacity: float32 [64, 256, 256], P('space'), may hold values from 0.5 to 2
- source: float32 [64, 256, 256], P('space'), may hold values from -6 to 6
- control: float32 [8, 16], P('tm'), may hold values from -2 to 2
- segment_index: int32 [64, 256], P('space'), may hold values from 0 to 15
Outputs:
- slice_ends: float32 [8, 64, 256, 256], P('tm', 'space')
The draws below stay inside these ranges and needn't reach their ends.
All inputs are finite; a program needn't handle non-finite values.
Results may differ from the reference program's by a relative error of at most 0.0001.
Values sent between devices are 32-bit elements; how exact they have to be, the bound alone decides.
No kernel may reach another device: no remote copies, remote signals or barrier semaphores. Data moves between devices by JAX's collectives and lax.ppermute only.
A program may use at most 64 MiB of HBM per device.

```python
import math
import jax
import jax.numpy as jnp

NY = 256
NZ = 256
FINE = 1
SWEEPS = 6
CORRECTIONS = 2
SEGMENTS = 16
SLICES = 8
NX = 64


def touch_ends(result, key, smallest, high):
    longest = result.shape.index(max(result.shape))
    spots = []
    for shift in (0, 1):
        where = [jax.random.randint(jax.random.fold_in(key, axis), (), 0, length) for axis, length in enumerate(result.shape)]
        where[longest] = (where[longest] + shift) % result.shape[longest]
        spots.append(tuple(where))
    return result.at[spots[0]].set(smallest).at[spots[1]].set(high)


def block_levels(rng, dims, shards, least, top_value):
    gain, own = 1.0, jax.random.fold_in(rng, 6)
    for dim, blocks in shards:
        steps = jnp.exp(jax.random.uniform(jax.random.fold_in(own, dim), (blocks,), jnp.float32, least / len(shards), top_value / len(shards)))
        gain = gain * jnp.repeat(steps, dims[dim] // blocks).reshape([-1 if axis == dim else 1 for axis in range(len(dims))])
    return gain


def centred(stream_key, extent, spread, most, cuts=(), kind=jnp.bfloat16):
    result = spread * jax.random.normal(stream_key, extent, jnp.float32)
    if cuts:
        result = result * block_levels(stream_key, extent, cuts, -0.22, 0.18)
    return jnp.clip(result, -most, most).astype(kind)


def setup_inputs(seed: int = 0) -> dict:
    keys = jax.random.split(jax.random.key(seed), 6)
    return {
        "initial_state": centred(keys[0], (NX, NY, NZ), 1.0, 6.0, ((0, 32),), jnp.float32),
        "capacity": jnp.clip(jnp.exp(math.log(2.0) - 1.3862944 * jax.random.uniform(keys[1], (NX, NY, NZ), jnp.float32) ** block_levels(keys[1], (NX, NY, NZ), ((0, 32),), -0.2, 0.2)), 0.5, 2.0),
        "source": centred(keys[2], (NX, NY, NZ), 1.0, 6.0, ((0, 32),), jnp.float32),
        "control": jnp.clip(jax.random.uniform(keys[3], (SLICES, SEGMENTS), jnp.float32, -2.0, 2.0) * block_levels(keys[3], (SLICES, SEGMENTS), ((0, 8),), -0.4, 0.0), -2.0, 2.0),
        "segment_index": touch_ends(jax.random.randint(keys[4], (NX, NZ), 0, SEGMENTS), jax.random.fold_in(keys[4], 1), 0, SEGMENTS - 1).astype(jnp.int32),
    }


step_fine = 1.0
step_coarse = 0.08


def neighbours(extended):
    core = extended[1:-1]
    total = extended[2:] + extended[:-2]
    wide = jnp.pad(core, ((0, 0), (1, 1), (0, 0)))
    total = total + wide[:, 2:] + wide[:, :-2]
    deeper = jnp.pad(core, ((0, 0), (0, 0), (1, 1)))
    return total + deeper[:, :, 2:] + deeper[:, :, :-2]


def jacobi_sweep(extended, previous, capacity, forcing, divisor):
    return (capacity * previous + step_fine * forcing + step_fine * neighbours(extended)) / divisor


def coarse_step(extended, scale, forcing):
    core = extended[1:-1]
    return core + scale * (neighbours(extended) - 6.0 * core + forcing)


def pad_planes(field):
    return jnp.pad(field, ((1, 1), (0, 0), (0, 0)))


def boundary_forcing(source, segment_index, control_row):
    matches = segment_index[:, None, :] == jnp.arange(SEGMENTS, dtype=jnp.int32)[None, :, None]
    values = jnp.sum(jnp.where(matches, control_row[None, :, None], jnp.zeros((), source.dtype)), axis=1)
    return source + jnp.pad(values[:, None, :], ((0, 0), (0, source.shape[1] - 1), (0, 0)))


def reference(initial_state, capacity, source, control, segment_index):
    divisor = capacity + 6.0 * step_fine
    scale = step_coarse / capacity
    forcings = [boundary_forcing(source, segment_index, control[slice_index]) for slice_index in range(SLICES)]

    def fine_solve(state, forcing):
        for fine_index in range(FINE):
            iterate = state
            for sweep_index in range(SWEEPS):
                iterate = jacobi_sweep(pad_planes(iterate), state, capacity, forcing, divisor)
            state = iterate
        return state

    starts = [initial_state]
    coarse_values = []
    for slice_index in range(SLICES):
        value = coarse_step(pad_planes(starts[slice_index]), scale, forcings[slice_index])
        coarse_values.append(value)
        if slice_index + 1 < SLICES:
            starts.append(value)
    ends = []
    for correction_index in range(CORRECTIONS):
        deltas = [fine_solve(starts[n], forcings[n]) - coarse_values[n] for n in range(SLICES)]
        new_starts = [initial_state]
        new_values = []
        ends = []
        for slice_index in range(SLICES):
            value = coarse_step(pad_planes(new_starts[slice_index]), scale, forcings[slice_index])
            new_values.append(value)
            end_state = value + deltas[slice_index]
            ends.append(end_state)
            if slice_index + 1 < SLICES:
                new_starts.append(end_state)
        starts = new_starts
        coarse_values = new_values
    return jnp.stack(ends)
```

```python
import jax
import jax.numpy as jnp
import numpy as np
from jax import lax
from jax.experimental import pallas as pl
from jax.experimental.pallas import tpu as pltpu
from jax.sharding import Mesh
from jax.sharding import PartitionSpec as P

SWEEPS = 6
SLICES = 8
SEGMENTS = 16
COARSE = 0.08
AXES = ("tm", "chip", "core")
CHIPS = 16
PLANES = 38
ROWS = 72
OWN = 24
LANES = 128
REACH = 17


def device_pairs(target):
    pairs = []
    for t in range(8):
        for chip in range(CHIPS):
            for core in range(2):
                to = target(chip, core)
                if to is None or not 0 <= to[0] < CHIPS:
                    continue
                t_to = t if chip // 8 == to[0] // 8 else t ^ 4
                pairs.append(((t * CHIPS + chip) * 2 + core, (t_to * CHIPS + to[0]) * 2 + to[1]))
    return pairs


PARTNER = device_pairs(lambda chip, core: (chip, 1 - core))
OUTWARD = device_pairs(lambda chip, core: (chip + 1 - 2 * core, core))
OUTWARD_5 = device_pairs(lambda chip, core: (chip + 5 - 10 * core, core))
FACING = device_pairs(lambda chip, core: (chip - 1 + 2 * core, 1 - core))
FACING_SAME = device_pairs(lambda chip, core: (chip - 1 + 2 * core, core))


def send(x, pairs):
    return lax.ppermute(x, AXES, pairs)


def lane_order():
    order = np.zeros((256, 256), np.float32)
    for z in range(256):
        order[z, (z % 2) * LANES + z // 2] = 1.0
    return order


def tiles(r):
    out = {}
    for i in range(r + 2):
        rho = -(-(r - max(0, i - 1)) // 4)
        for k in range(2 + rho):
            out.setdefault(OWN - 4 * rho + 8 * k, []).append(i)
    return sorted(out.items())


def main_kernel(meta, steps, own_c, own_q, near_c, near_q, far_c, far_q, end_cq, pnear_c, pnear_q, pfar_c, pfar_q,
                pend_cq, order, out, sig, rd, q, va, vb, wa, wb, ua, ub, e, le, ha, hb, total, jumps, segs, ends, sems):
    core = meta[0]
    zero = meta[1]

    copies = []

    def copy(src, dst):
        c = pltpu.make_async_copy(src, dst, sems.at[len(copies)])
        c.start()
        copies.append(c)

    half = pl.multiple_of(core * 16, 8)
    for own, near, far, end, pnear, pfar, pend, dst in (
        (own_c, near_c, far_c, 0, pnear_c, pfar_c, 0, sig),
        (own_q, near_q, far_q, 1, pnear_q, pfar_q, 1, q),
    ):
        copy(own.at[:, :, pl.ds(half, 64), :], dst.at[pl.ds(REACH, 4), :, pl.ds(0, 64), :])
        for block, blocks, end_block, mine in ((near, far, end_cq, True), (pnear, pfar, pend_cq, False)):
            side = core if mine else 1 - core
            for k in range(1, 5):
                p = REACH - 4 * k + side * (8 * k)
                if k <= 2:
                    b = block.at[k - 1]
                    copy(b.at[:, :, pl.ds(half, 48), :], dst.at[pl.ds(p, 4), :, pl.ds(OWN - 16, 48), :])
                    if k == 1 and dst is q:
                        copy(b.at[:, :, pl.ds(8, 8), :], dst.at[pl.ds(p, 4), :, pl.ds(0, 8), :])
                else:
                    b = blocks.at[k - 3]
                    copy(b.at[:, :, pl.ds(half, 32), :], dst.at[pl.ds(p, 4), :, pl.ds(OWN - 8, 32), :])
            copy(end_block.at[end, :, pl.ds(half, 32), :],
                 dst.at[(PLANES - 1) * side, :, pl.ds(OWN - 8, 32), :])
    for c in copies:
        c.wait()

    lane = lax.broadcasted_iota(jnp.int32, (8, LANES), 1)
    row = lax.broadcasted_iota(jnp.int32, (8, LANES), 0)
    first, last = lane == 0, lane == LANES - 1

    def take_segments(p, _):
        for h in range(2):
            segs[h, pl.ds(p, 1), :] = q[p, h, pl.ds(16 * (1 - core), 1), :]
        return 0

    lax.fori_loop(0, PLANES, take_segments, 0)
    for h in range(2):
        s = segs[h]
        acc = [jnp.zeros_like(s) for _ in range(SLICES)]
        for m in range(SEGMENTS):
            hit = s == jnp.float32(m)
            acc = [jnp.where(hit, steps[n, m], a) for n, a in enumerate(acc)]
        for n in range(SLICES):
            jumps[0, n, h] = acc[n] * steps[SLICES, 0]
            if n < 2:
                jumps[1, n, h] = acc[n] * steps[SLICES, 1]

    def on_sides(*stages):
        def body(side, _):
            plane = [18 + side + (2 * side - 1) * i for i in range(-1, REACH + 2)]
            stores = []
            for stage in stages:
                stage(lambda i: plane[i + 1], stores)
            for ref, p, h, y, value in stores:
                ref[p, h, pl.ds(y, 8), :] = value
            return 0

        lax.fori_loop(0, 2, body, 0)

    def loader(plane):
        cache = {}

        def load(ref, i, h, y):
            key = (id(ref), i, h, y)
            if key not in cache:
                cache[key] = ref[plane(i), h, pl.ds(zero + y, 8), :]
            return cache[key]

        return load

    def around(ref, plane, load, i, y):
        even, odd = load(ref, i, 0, y), load(ref, i, 1, y)
        z = (odd + jnp.where(first, 0.0, pltpu.roll(odd, 1, 1)), even + jnp.where(last, 0.0, pltpu.roll(even, LANES - 1, 1)))
        sums = []
        for h in range(2):
            sums.append(z[h] + (load(ref, i, h, y - 1) + load(ref, i, h, y + 1))
                        + (load(ref, i - 1, h, y) + load(ref, i + 1, h, y)))
        return sums

    def jump(plane, n, i, h, y):
        result = None
        for which, at in ((0, OWN), (1, OWN - 16)):
            if y <= at < y + 8 and (which == 0 or n < 2):
                value = jnp.where(row == at - y, jumps[which, n, h, pl.ds(plane(i), 1), :], 0.0)
                result = value if result is None else result + value
        return result

    def setup(plane, stores):
        load = loader(plane)
        for y, planes in tiles(17):
            for i in planes:
                for h in range(2):
                    c = load(sig, i, h, y)
                    inside = c > 0.0
                    c = jnp.where(inside, c, 1.0)
                    s = jnp.where(inside, COARSE / c, 0.0)
                    d = jnp.where(inside, 1.0 / (c + 6.0), 0.0)
                    value = load(q, i, h, y)
                    change = jump(plane, 0, i, h, y)
                    p = plane(i)
                    if change is not None:
                        value = value + change
                        stores.append((q, p, h, zero + y, value))
                    stores += [(sig, p, h, zero + y, s), (rd, p, h, zero + y, d), (va, p, h, zero + y, s * value),
                               (wa, p, h, zero + y, d * value)]

    def advance(n, r, v_old, v_new):
        def stage(plane, stores):
            load = loader(plane)
            for y, planes in tiles(r):
                for i in planes:
                    sums = around(v_old, plane, load, i, y)
                    for h in range(2):
                        value = load(q, i, h, y) + (sums[h] - 6.0 * load(v_old, i, h, y))
                        change = jump(plane, n, i, h, y)
                        if change is not None:
                            value = value + change
                        p = plane(i)
                        stores.append((q, p, h, zero + y, value))
                        if n < SLICES - 1:
                            stores += [(v_new, p, h, zero + y, load(sig, i, h, y) * value),
                                       (wa, p, h, zero + y, load(rd, i, h, y) * value)]
        return stage

    def second_order(n, r):
        def stage(plane, stores):
            load = loader(plane)
            for y, planes in tiles(r):
                for i in planes:
                    sums = around(e, plane, load, i, y)
                    for h in range(2):
                        value = sums[h] - 6.0 * load(e, i, h, y)
                        p = plane(i)
                        stores += [(le, p, h, zero + y, value), (ua, p, h, zero + y, load(rd, i, h, y) * value)]
        return stage

    def with_source(plane, stores):
        load = loader(plane)
        for y, planes in tiles(5):
            for i in planes:
                for h in range(2):
                    value = load(le, i, h, y) + load(q, i, h, y)
                    p = plane(i)
                    stores += [(le, p, h, zero + y, value), (ua, p, h, zero + y, load(rd, i, h, y) * value)]

    def sweep(r, src, dst, source):
        def stage(plane, stores):
            load = loader(plane)
            for y, planes in tiles(r):
                for i in planes:
                    sums = around(src, plane, load, i, y)
                    for h in range(2):
                        stores.append((dst, plane(i), h, zero + y, load(rd, i, h, y) * (load(source, i, h, y) + sums[h])))
        return stage

    def finish_first(n, r, src):
        def stage(plane, stores):
            load = loader(plane)
            for y, planes in tiles(r):
                for i in planes:
                    sums = around(src, plane, load, i, y)
                    for h in range(2):
                        value = load(rd, i, h, y) * (load(q, i, h, y) + sums[h])
                        s = load(sig, i, h, y)
                        if n == 0:
                            value = value - s * load(q, i, h, y)
                        else:
                            value = load(e, i, h, y) + (value + s * (load(le, i, h, y) - load(q, i, h, y)))
                        stores.append((e, plane(i), h, zero + y, value))
        return stage

    def finish_second(n, r, src, h_old, h_new):
        def stage(plane, stores):
            load = loader(plane)
            for y, planes in tiles(r):
                for i in planes:
                    sums = around(src, plane, load, i, y)
                    around_h = around(h_old, plane, load, i, y) if n > 1 else None
                    for h in range(2):
                        value = load(rd, i, h, y) * (load(le, i, h, y) + sums[h])
                        s = load(sig, i, h, y)
                        coarse = None
                        if n > 1:
                            coarse = around_h[h] - 6.0 * load(h_old, i, h, y)
                        if n < SLICES - 1:
                            own = load(le, i, h, y)
                            coarse = -own if coarse is None else coarse - own
                        value = value + s * coarse
                        if n > 1:
                            value = load(h_old, i, h, y) + value
                        if n < SLICES - 1:
                            stores.append((h_new, plane(i), h, zero + y, value))
                        else:
                            emit(plane, stores, n, i, h, y, load(total, plane(i) - REACH - i + i, h, y) if False else None, value)
        return stage

    def emit(plane, stores, n, i, h, y, _, value):
        p = plane(i) - REACH
        value = value + total[p, h, pl.ds(y - OWN, 8), :] + e[plane(i), h, pl.ds(y, 8), :]
        stores.append((ends, n * 4 + p, h, y - OWN, value))

    def close(n, v):
        def stage(plane, stores):
            for y, planes in tiles(0):
                for i in planes:
                    for h in range(2):
                        p = plane(i) - REACH
                        value = v[plane(i), h, pl.ds(y, 8), :]
                        if n > 0:
                            value = value + total[p, h, pl.ds(y - OWN, 8), :]
                        stores.append((total, p, h, y - OWN, value))
                        value = value + e[plane(i), h, pl.ds(y, 8), :]
                        if n > 0:
                            h_now = ha if n % 2 == 0 else hb
                            value = value + h_now[plane(i), h, pl.ds(y, 8), :]
                        stores.append((ends, n * 4 + p, h, y - OWN, value))
        return stage

    on_sides(setup)
    v_now, v_next = va, vb
    for n in range(SLICES):
        if n > 0:
            stages = [close(n - 1, v_now), second_order(n, min(12 - n, 12))]
            r = 17 - n if n < SLICES - 1 else 5
            stages.append(advance(n, r, v_now, v_next))
            on_sides(*stages)
            v_now, v_next = v_next, v_now
            if n == SLICES - 1:
                on_sides(with_source)
        w_src, w_dst, u_src, u_dst = wa, wb, ua, ub
        for k in range(2, SWEEPS + 1):
            stages = []
            if n < SLICES - 1:
                r = 18 - n - k
                stages.append(sweep(r, w_src, w_dst, q) if k < SWEEPS else finish_first(n, r, w_src))
            if n > 0:
                r = 13 - n - k
                if k < SWEEPS:
                    stages.append(sweep(r, u_src, u_dst, le))
                else:
                    h_old, h_new = (ha, hb) if n % 2 == 1 else (hb, ha)
                    stages.append(finish_second(n, r, u_src, h_old, h_new))
            on_sides(*stages)
            w_src, w_dst, u_src, u_dst = w_dst, w_src, u_dst, u_src

    for n in range(SLICES):
        for p in range(4):
            tile = ends[n * 4 + p]
            both = jnp.concatenate([tile[0], tile[1]], axis=1)
            out[n, p] = lax.dot_general(both, order[...], (((1,), (1,)), ((), ())), precision=lax.Precision.HIGHEST,
                                        preferred_element_type=jnp.float32)


def solve(meta, steps, *blocks):
    field = pltpu.VMEM((PLANES, 2, ROWS, LANES), jnp.float32)
    order = jnp.asarray(lane_order())
    any_space = pl.BlockSpec(memory_space=pl.ANY)
    smem = pl.BlockSpec(memory_space=pltpu.SMEM)
    vmem = pl.BlockSpec(memory_space=pltpu.VMEM)
    return pl.pallas_call(
        main_kernel,
        out_shape=jax.ShapeDtypeStruct((SLICES, 4, 16, 256), jnp.float32),
        in_specs=[smem, smem] + [any_space] * len(blocks) + [vmem],
        out_specs=vmem,
        scratch_shapes=[field] * 13 + [
            pltpu.VMEM((4, 2, 16, LANES), jnp.float32),
            pltpu.VMEM((2, SLICES, 2, 40, LANES), jnp.float32),
            pltpu.VMEM((2, 40, LANES), jnp.float32),
            pltpu.VMEM((SLICES * 4, 2, 16, LANES), jnp.float32),
            pltpu.SemaphoreType.DMA((32,)),
        ],
        compiler_params=pltpu.CompilerParams(vmem_limit_bytes=60 << 20),
        name="parareal",
    )(meta, steps, *blocks, order)


def on_device(initial_state, capacity, source, control, segment_index):
    tm, chip, core = lax.axis_index("tm"), lax.axis_index("chip"), lax.axis_index("core")
    block = jnp.where(chip >= CHIPS // 2, tm ^ 4, tm)
    controls = lax.all_gather(control, "tm", axis=0, tiled=True)

    above = jnp.zeros((2, 25, 256), jnp.float32)
    marked = above.at[:, 17, :].set(segment_index.astype(jnp.float32))

    def window(x, top):
        return lax.dynamic_slice_in_dim(jnp.concatenate([top, x, above], axis=1), 32 * block, 82, axis=1)

    mine = jnp.stack([window(capacity, above), window(source, marked), window(initial_state, above)])
    theirs = send(mine, PARTNER)
    outer = jnp.where(core == 0, mine[2, 0], mine[2, 1])
    facing = send(outer, FACING)
    facing_same = send(outer, FACING_SAME)
    chip4 = jnp.where(core == 0, jnp.concatenate([mine, theirs], axis=1), jnp.concatenate([theirs, mine], axis=1))
    before = jnp.where(core == 0, facing, facing_same)
    after = jnp.where(core == 0, facing_same, facing)
    state = jnp.concatenate([before[None], chip4[2], after[None]], axis=0)
    middle = state[1:-1, 1:-1]
    deeper = jnp.pad(middle, ((0, 0), (0, 0), (1, 1)))
    residual = (state[2:, 1:-1] + state[:-2, 1:-1] + state[1:-1, 2:] + state[1:-1, :-2]
                + deeper[:, :, 2:] + deeper[:, :, :-2] - 6.0 * middle + chip4[1, :, 1:-1])
    order = jnp.asarray(lane_order())

    def laid(x):
        return jnp.stack([jnp.dot(x, order[:, h * LANES:(h + 1) * LANES], precision=lax.Precision.HIGHEST)
                          for h in range(2)], axis=1)

    own_c, own_q = laid(chip4[0, :, 1:-1]), laid(residual)
    x_c, x_q = own_c[:, :, 8:72], own_q[:, :, 8:72]
    near, far = [], []
    for k in range(4):
        if k == 2:
            x_c, x_q = x_c[:, :, 8:56], x_q[:, :, 8:56]
        x_c, x_q = send(x_c, OUTWARD), send(x_q, OUTWARD)
        (near if k < 2 else far).append((x_c, x_q))
    edge = jnp.stack([own_c, own_q])[:, :, :, 16:64]
    end_cq = send(jnp.where(core == 0, edge[:, 3], edge[:, 0]), OUTWARD_5)
    near_c, near_q = (jnp.stack([b[j] for b in near]) for j in range(2))
    far_c, far_q = (jnp.stack([b[j] for b in far]) for j in range(2))
    got = (near_c, near_q, far_c, far_q, end_cq)
    passed = tuple(send(x, PARTNER) for x in got)

    first = jnp.where(block == 0, 1.0, 0.0)
    changes = jnp.concatenate([controls[:1], controls[1:] - controls[:-1]], axis=0) * first
    flags = jnp.zeros((1, SEGMENTS), jnp.float32).at[0, 0].set(jnp.where(core == 0, 1.0, 0.0)).at[0, 1].set(
        jnp.where(core == 1, 1.0, 0.0))
    steps = jnp.concatenate([changes, flags], axis=0)
    meta = jnp.stack([core.astype(jnp.int32), (core * 0).astype(jnp.int32)])
    ends = solve(meta, steps, own_c, own_q, *got, *passed)

    split = ends.reshape(SLICES * 2, 2, 16, 256)
    mixed = lax.all_to_all(split, ("tm", "core"), split_axis=0, concat_axis=0, tiled=True).reshape(2, 4, 2, 2, 16, 256)
    mixed = jnp.where(chip >= CHIPS // 2, mixed[::-1], mixed)
    whole = mixed.transpose(3, 0, 1, 2, 4, 5).reshape(2, 256, 256)
    return (whole + initial_state)[None]


def solution(mesh):
    split = Mesh(mesh.devices.reshape(8, CHIPS, 2), AXES)
    space = ("chip", "core")
    in_specs = (P(space, None, None), P(space, None, None), P(space, None, None), P("tm", None), P(space, None))
    return jax.shard_map(on_device, mesh=split, in_specs=in_specs, out_specs=P("tm", space, None, None), check_vma=False)
```

```python
import jax
import jax.numpy as jnp
import numpy as np
from jax import lax
from jax.experimental import pallas as pl
from jax.experimental.pallas import tpu as pltpu
from jax.sharding import Mesh
from jax.sharding import PartitionSpec as P

SWEEPS = 6
SLICES = 8
SEGMENTS = 16
COARSE = 0.08
AXES = ("tm", "chip", "core")
CHIPS = 16
PLANES = 38
ROWS = 72
OWN = 24
MOST = 112
LANES = 128
REACH = 17


def device_pairs(target):
    pairs = []
    for t in range(8):
        for chip in range(CHIPS):
            for core in range(2):
                to = target(chip, core)
                if to is None or not 0 <= to[0] < CHIPS:
                    continue
                t_to = t if chip // 8 == to[0] // 8 else t ^ 4
                pairs.append(((t * CHIPS + chip) * 2 + core, (t_to * CHIPS + to[0]) * 2 + to[1]))
    return pairs


PARTNER = device_pairs(lambda chip, core: (chip, 1 - core))
OUTWARD = device_pairs(lambda chip, core: (chip + 1 - 2 * core, core))
OUTWARD_5 = device_pairs(lambda chip, core: (chip + 5 - 10 * core, core))
FACING = device_pairs(lambda chip, core: (chip - 1 + 2 * core, 1 - core))
FACING_SAME = device_pairs(lambda chip, core: (chip - 1 + 2 * core, core))


def send(x, pairs):
    return lax.ppermute(x, AXES, pairs)


def lane_order():
    order = np.zeros((256, 256), np.float32)
    for z in range(256):
        order[z, (z % 2) * LANES + z // 2] = 1.0
    return order


def tiles(r):
    out = {}
    for p in range(REACH - r, REACH + 4 + r):
        rho = -(-(r - max(0, REACH - p, p - REACH - 3)) // 4)
        for k in range(2 + rho):
            out.setdefault(OWN - 4 * rho + 8 * k, []).append(p)
    return sorted(out.items())


def main_kernel(controls, *refs):
    (own_c, own_q), blocks, (order, out) = refs[:2], refs[2:20], refs[20:22]
    sig, rd, q, v, wa, wb, ua, ub, e, le, hh, total, jumps, segs, ends, sems = refs[22:]
    core, chip, tm = lax.axis_index("core"), lax.axis_index("chip"), lax.axis_index("tm")
    zero = tm >> 5
    trips = zero + 1
    at_edge = jnp.where(chip >= CHIPS // 2, tm ^ 4, tm) == 0

    copies = []

    def copy(src, dst):
        c = pltpu.make_async_copy(src, dst, sems.at[len(copies)])
        c.start()
        copies.append(c)

    half = pl.multiple_of(core * 16, 8)
    for f, (own, dst) in enumerate(((own_c, sig), (own_q, q))):
        copy(own.at[:, :, pl.ds(half, 64), :], dst.at[pl.ds(REACH, 4), :, pl.ds(0, 64), :])
        for mine in range(2):
            side = 1 - core if mine == 1 else core
            group = blocks[9 * mine:9 * mine + 9]
            for k in range(1, 5):
                b = group[2 * (k - 1) + f]
                p = REACH - 4 * k + side * (8 * k)
                if k <= 2:
                    copy(b.at[:, :, pl.ds(half, 48), :], dst.at[pl.ds(p, 4), :, pl.ds(OWN - 16, 48), :])
                    if k == 1 and f == 1:
                        copy(b.at[:, :, pl.ds(8, 8), :], dst.at[pl.ds(p, 4), :, pl.ds(0, 8), :])
                else:
                    copy(b.at[:, :, pl.ds(half, 32), :], dst.at[pl.ds(p, 4), :, pl.ds(OWN - 8, 32), :])
            copy(group[8].at[f, :, pl.ds(half, 32), :], dst.at[(PLANES - 1) * side, :, pl.ds(OWN - 8, 32), :])
    for c in copies:
        c.wait()

    lane = lax.broadcasted_iota(jnp.int32, (8, LANES), 1)
    row = lax.broadcasted_iota(jnp.int32, (8, LANES), 0)
    first, last = lane == 0, lane == LANES - 1

    def take_segments(p, _):
        for h in range(2):
            segs[h, pl.ds(p, 1), :] = q[p, h, pl.ds(16 * (1 - core), 1), :]
        return 0

    lax.fori_loop(0, PLANES, take_segments, 0)
    here = [jnp.where(at_edge & (core == c), 1.0, 0.0) for c in range(2)]
    for h in range(2):
        s = segs[h]
        acc = [jnp.zeros_like(s) for _ in range(SLICES)]
        for m in range(SEGMENTS):
            hit = s == jnp.float32(m)
            for n in range(SLICES):
                change = controls[n, m] - controls[n - 1, m] if n > 0 else controls[n, m]
                acc[n] = jnp.where(hit, change, acc[n])
        for n in range(SLICES):
            jumps[0, n, h] = acc[n] * here[0]
            if n < 3:
                jumps[1, n, h] = acc[n] * here[1] if n < 2 else jnp.zeros_like(s)

    def step(*stages):
        blocks, room = [], 0
        for stage, part in stages:
            part = list(part)
            while part:
                if room < 8:
                    blocks.append([])
                    room = MOST
                blocks[-1].append((stage, part[:room]))
                part, room = part[room:], room - min(room, len(part))
        for block in blocks:
            def body(_, carry, block=block):
                stores = []
                for stage, part in block:
                    stage(stores, part)
                for ref, p, h, y, value in stores:
                    ref[p, h, pl.ds(y, 8), :] = value
                return carry

            lax.fori_loop(0, trips, body, 0)

    def loader():
        cache = {}

        def load(ref, p, h, y, base=0):
            key = (id(ref), p, h, y)
            if key not in cache:
                cache[key] = ref[base + p, h, pl.ds(zero + y, 8), :]
            return cache[key]

        return load

    def around(ref, load, p, y, base=0):
        even, odd = load(ref, p, 0, y, base), load(ref, p, 1, y, base)
        z = (odd + jnp.where(first, 0.0, pltpu.roll(odd, 1, 1)), even + jnp.where(last, 0.0, pltpu.roll(even, LANES - 1, 1)))
        return [z[h] + (load(ref, p, h, y - 1, base) + load(ref, p, h, y + 1, base))
                + (load(ref, p - 1, h, y, base) + load(ref, p + 1, h, y, base)) for h in range(2)]

    def cells(r):
        for y, planes in tiles(r):
            for p in planes:
                yield y, p

    def jump(n, p, h, y, both):
        result = None
        for which, at in ((0, OWN), (1, OWN - 16)):
            if y <= at < y + 8 and (which == 0 or both):
                value = jnp.where(row == at - y, jumps[which, n, h, pl.ds(p, 1), :], 0.0)
                result = value if result is None else result + value
        return result

    def setup(stores, part):
        load = loader()
        for y, p in part:
            for h in range(2):
                c = load(sig, p, h, y)
                inside = c > 0.0
                c = jnp.where(inside, c, 1.0)
                s = jnp.where(inside, COARSE / c, 0.0)
                d = jnp.where(inside, 1.0 / (c + 6.0), 0.0)
                value = load(q, p, h, y)
                change = jump(0, p, h, y, True)
                if change is not None:
                    value = value + change
                    stores.append((q, p, h, zero + y, value))
                stores += [(sig, p, h, zero + y, s), (rd, p, h, zero + y, d), (v, p, h, zero + y, s * value),
                           (wa, p, h, zero + y, d * value)]

    def clear(stores, part):
        nothing = jnp.zeros((8, LANES), jnp.float32)
        for p in range(REACH - 7, REACH + 11):
            for h in range(2):
                for y in range(OWN - 16, OWN + 32, 8):
                    stores.append((hh, p, h, y, nothing))
        for p in range(4):
            for h in range(2):
                stores += [(total, p, h, 0, nothing), (total, p, h, 8, nothing)]

    def advance(n, r, old, new, both):
        def stage(stores, part):
            load = loader()
            for y, p in part:
                sums = around(v, load, p, y, old)
                for h in range(2):
                    value = load(q, p, h, y) + (sums[h] - 6.0 * load(v, p, h, y))
                    change = jump(n, p, h, y, both)
                    if change is not None:
                        value = value + change
                    stores.append((q, p, h, zero + y, value))
                    if new is not None:
                        stores += [(v, new + p, h, zero + y, load(sig, p, h, y) * value),
                                   (wa, p, h, zero + y, load(rd, p, h, y) * value)]
        return stage, cells(r)

    def second_order(r):
        def stage(stores, part):
            load = loader()
            for y, p in part:
                sums = around(e, load, p, y)
                for h in range(2):
                    value = sums[h] - 6.0 * load(e, p, h, y)
                    stores += [(le, p, h, zero + y, value), (ua, p, h, zero + y, load(rd, p, h, y) * value)]
        return stage, cells(r)

    def with_source(stores, part):
        load = loader()
        for y, p in part:
            for h in range(2):
                value = load(le, p, h, y) + load(q, p, h, y)
                stores += [(le, p, h, zero + y, value), (ua, p, h, zero + y, load(rd, p, h, y) * value)]

    def sweep(r, src, dst, source):
        def stage(stores, part):
            load = loader()
            for y, p in part:
                sums = around(src, load, p, y)
                for h in range(2):
                    stores.append((dst, p, h, zero + y, load(rd, p, h, y) * (load(source, p, h, y) + sums[h])))
        return stage, cells(r)

    def finish_first(initial, r, src):
        def stage(stores, part):
            load = loader()
            for y, p in part:
                sums = around(src, load, p, y)
                for h in range(2):
                    value = load(rd, p, h, y) * (load(q, p, h, y) + sums[h])
                    s = load(sig, p, h, y)
                    if initial:
                        value = value - s * load(q, p, h, y)
                    else:
                        value = load(e, p, h, y) + (value + s * (load(le, p, h, y) - load(q, p, h, y)))
                    stores.append((e, p, h, zero + y, value))
        return stage, cells(r)

    def finish_second(r, src, old, new):
        def stage(stores, part):
            load = loader()
            for y, p in part:
                sums = around(src, load, p, y)
                around_h = around(hh, load, p, y, old)
                for h in range(2):
                    value = load(rd, p, h, y) * (load(le, p, h, y) + sums[h])
                    coarse = around_h[h] - 6.0 * load(hh, p, h, y)
                    if new is not None:
                        coarse = coarse - load(le, p, h, y)
                    value = load(hh, p, h, y) + (value + load(sig, p, h, y) * coarse)
                    if new is not None:
                        stores.append((hh, new + p, h, zero + y, value))
                    else:
                        value = value + total[p - REACH, h, pl.ds(y - OWN, 8), :] + load(e, p, h, y)
                        stores.append((ends, (SLICES - 1) * 4 + p - REACH, h, y - OWN, value))
        return stage, cells(r)

    def close(n, old):
        def stage(stores, part):
            for y, p in part:
                for h in range(2):
                    value = v[old + p, h, pl.ds(y, 8), :] + total[p - REACH, h, pl.ds(y - OWN, 8), :]
                    stores.append((total, p - REACH, h, y - OWN, value))
                    value = value + e[p, h, pl.ds(y, 8), :] + hh[old + p, h, pl.ds(y, 8), :]
                    stores.append((ends, (n - 1) * 4 + p - REACH, h, y - OWN, value))
        return stage, cells(0)

    def sweeps(n, r_w, r_u, old, new, initial=False):
        w, u = (wa, wb), (ua, ub)
        for k in range(SWEEPS - 1):
            stages = []
            if r_w is not None:
                stages.append(sweep(r_w - k, *w, q) if k < SWEEPS - 2 else finish_first(initial, r_w - k, w[0]))
            if r_u is not None:
                stages.append(sweep(r_u - k, *u, le) if k < SWEEPS - 2 else finish_second(r_u - k, u[0], old, new))
            step(*stages)
            w, u = w[::-1], u[::-1]

    step((setup, cells(17)), (clear, [None]))
    sweeps(0, 16, None, None, None, True)
    for start in range(1, SLICES - 1, 2):
        def slice_pair(j, carry, start=start):
            n = start + j
            old, new = PLANES * j, PLANES * (1 - j)
            step(close(n, old), second_order(12 - start), advance(n, 17 - start, old, new, start == 1))
            sweeps(n, 16 - start, 11 - start, old, new)
            return carry

        lax.fori_loop(0, 2, slice_pair, 0)
    step(close(SLICES - 1, 0), second_order(5), advance(SLICES - 1, 5, 0, None, False))
    step((with_source, cells(5)))
    sweeps(SLICES - 1, None, 4, 0, None)

    both = jnp.concatenate([ends[:, h].reshape(SLICES * 4 * 16, LANES) for h in range(2)], axis=1)
    whole = lax.dot_general(both, order[...], (((1,), (1,)), ((), ())), precision=lax.Precision.HIGHEST,
                            preferred_element_type=jnp.float32)
    out[...] = whole.reshape(SLICES, 4, 16, 256)


def solve(controls, *blocks):
    field = pltpu.VMEM((PLANES, 2, ROWS, LANES), jnp.float32)
    two = pltpu.VMEM((2 * PLANES, 2, ROWS, LANES), jnp.float32)
    any_space = pl.BlockSpec(memory_space=pl.ANY)
    smem = pl.BlockSpec(memory_space=pltpu.SMEM)
    vmem = pl.BlockSpec(memory_space=pltpu.VMEM)
    return pl.pallas_call(
        main_kernel,
        out_shape=jax.ShapeDtypeStruct((SLICES, 4, 16, 256), jnp.float32),
        in_specs=[smem] + [any_space] * len(blocks) + [vmem],
        out_specs=vmem,
        scratch_shapes=[field] * 3 + [two] + [field] * 6 + [two] + [
            pltpu.VMEM((4, 2, 16, LANES), jnp.float32),
            pltpu.VMEM((2, SLICES, 2, 40, LANES), jnp.float32),
            pltpu.VMEM((2, 40, LANES), jnp.float32),
            pltpu.VMEM((SLICES * 4, 2, 16, LANES), jnp.float32),
            pltpu.SemaphoreType.DMA((24,)),
        ],
        compiler_params=pltpu.CompilerParams(vmem_limit_bytes=60 << 20),
        name="parareal",
    )(controls, *blocks, jnp.asarray(lane_order()))


def on_device(initial_state, capacity, source, control, segment_index):
    tm, chip, core = lax.axis_index("tm"), lax.axis_index("chip"), lax.axis_index("core")
    block = jnp.where(chip >= CHIPS // 2, tm ^ 4, tm)
    controls = lax.all_to_all(jnp.broadcast_to(control, (SLICES, SEGMENTS)), "tm", split_axis=0, concat_axis=0, tiled=True)

    above = jnp.zeros((2, 25, 256), jnp.float32)
    marked = above.at[:, 17, :].set(segment_index.astype(jnp.float32))

    def window(x, top):
        return lax.dynamic_slice_in_dim(jnp.concatenate([top, x, above], axis=1), 32 * block, 82, axis=1)

    mine = jnp.stack([window(capacity, above), window(source, marked), window(initial_state, above)])
    theirs = send(mine, PARTNER)
    outer = jnp.where(core == 0, mine[2, 0], mine[2, 1])
    facing = send(outer, FACING)
    facing_same = send(outer, FACING_SAME)
    chip4 = jnp.where(core == 0, jnp.concatenate([mine, theirs], axis=1), jnp.concatenate([theirs, mine], axis=1))
    before = jnp.where(core == 0, facing, facing_same)
    after = jnp.where(core == 0, facing_same, facing)
    state = jnp.concatenate([before[None], chip4[2], after[None]], axis=0)
    middle = state[1:-1, 1:-1]
    deeper = jnp.pad(middle, ((0, 0), (0, 0), (1, 1)))
    residual = (state[2:, 1:-1] + state[:-2, 1:-1] + state[1:-1, 2:] + state[1:-1, :-2]
                + deeper[:, :, 2:] + deeper[:, :, :-2] - 6.0 * middle + chip4[1, :, 1:-1])
    order = jnp.asarray(lane_order())

    def laid(x):
        return jnp.stack([jnp.dot(x, order[:, h * LANES:(h + 1) * LANES], precision=lax.Precision.HIGHEST)
                          for h in range(2)], axis=1)

    own_c, own_q = laid(chip4[0, :, 1:-1]), laid(residual)
    x_c, x_q = own_c[:, :, 8:72], own_q[:, :, 8:72]
    got = []
    for k in range(4):
        if k == 2:
            x_c, x_q = x_c[:, :, 8:56], x_q[:, :, 8:56]
        x_c, x_q = send(x_c, OUTWARD), send(x_q, OUTWARD)
        got += [x_c, x_q]
    edge = jnp.stack([own_c, own_q])[:, :, :, 16:64]
    got.append(send(jnp.where(core == 0, edge[:, 3], edge[:, 0]), OUTWARD_5))
    passed = [send(x, PARTNER) for x in got]
    ends = solve(controls, own_c, own_q, *got, *passed)

    split = ends.reshape(SLICES * 2, 2, 16, 256)
    mixed = lax.all_to_all(split, ("tm", "core"), split_axis=0, concat_axis=0, tiled=True).reshape(2, 4, 2, 2, 16, 256)
    mixed = jnp.where(chip >= CHIPS // 2, mixed[::-1], mixed)
    whole = mixed.transpose(3, 0, 1, 2, 4, 5).reshape(2, 256, 256)
    return (whole + initial_state)[None]


def solution(mesh):
    split = Mesh(mesh.devices.reshape(8, CHIPS, 2), AXES)
    space = ("chip", "core")
    in_specs = (P(space, None, None), P(space, None, None), P(space, None, None), P("tm", None), P(space, None))
    return jax.shard_map(on_device, mesh=split, in_specs=in_specs, out_specs=P("tm", space, None, None), check_vma=False)
```

```python
import jax
import jax.numpy as jnp
import numpy as np
from jax import lax
from jax.experimental import pallas as pl
from jax.experimental.pallas import tpu as pltpu
from jax.sharding import Mesh
from jax.sharding import PartitionSpec as P

SWEEPS = 6
SLICES = 8
SEGMENTS = 16
COARSE = 0.08
AXES = ("tm", "chip", "core")
CHIPS = 16
PLANES = 38
ROWS = 72
OWN = 24
MOST = 112
LANES = 128
REACH = 17


def device_pairs(target):
    pairs = []
    for t in range(8):
        for chip in range(CHIPS):
            for core in range(2):
                to = target(chip, core)
                if to is None or not 0 <= to[0] < CHIPS:
                    continue
                t_to = t if chip // 8 == to[0] // 8 else t ^ 4
                pairs.append(((t * CHIPS + chip) * 2 + core, (t_to * CHIPS + to[0]) * 2 + to[1]))
    return pairs


PARTNER = device_pairs(lambda chip, core: (chip, 1 - core))
OUTWARD = device_pairs(lambda chip, core: (chip + 1 - 2 * core, core))
OUTWARD_5 = device_pairs(lambda chip, core: (chip + 5 - 10 * core, core))
FACING = device_pairs(lambda chip, core: (chip - 1 + 2 * core, 1 - core))
FACING_SAME = device_pairs(lambda chip, core: (chip - 1 + 2 * core, core))


def send(x, pairs):
    return lax.ppermute(x, AXES, pairs)


def lane_order():
    order = np.zeros((256, 256), np.float32)
    for z in range(256):
        order[z, (z % 2) * LANES + z // 2] = 1.0
    return order


def tiles(r):
    out = {}
    for p in range(REACH - r, REACH + 4 + r):
        rho = -(-(r - max(0, REACH - p, p - REACH - 3)) // 4)
        for k in range(2 + rho):
            out.setdefault(OWN - 4 * rho + 8 * k, []).append(p)
    return sorted(out.items())


def main_kernel(controls, *refs):
    (own_c, own_q), blocks, (order, out) = refs[:2], refs[2:20], refs[20:22]
    sig, rd, q, v, wa, wb, ua, ub, e, le, hh, total, jumps, segs, ends, sems = refs[22:]
    core, chip, tm = lax.axis_index("core"), lax.axis_index("chip"), lax.axis_index("tm")
    zero = tm >> 5
    trips = zero + 1
    at_edge = jnp.where(chip >= CHIPS // 2, tm ^ 4, tm) == 0

    copies = []

    def copy(src, dst):
        c = pltpu.make_async_copy(src, dst, sems.at[len(copies)])
        c.start()
        copies.append(c)

    half = pl.multiple_of(core * 16, 8)
    for f, (own, dst) in enumerate(((own_c, sig), (own_q, q))):
        copy(own.at[:, :, pl.ds(half, 64), :], dst.at[pl.ds(REACH, 4), :, pl.ds(0, 64), :])
        for mine in range(2):
            side = 1 - core if mine == 1 else core
            group = blocks[9 * mine:9 * mine + 9]
            for k in range(1, 5):
                b = group[2 * (k - 1) + f]
                p = REACH - 4 * k + side * (8 * k)
                if k <= 2:
                    copy(b.at[:, :, pl.ds(half, 48), :], dst.at[pl.ds(p, 4), :, pl.ds(OWN - 16, 48), :])
                    if k == 1 and f == 1:
                        copy(b.at[:, :, pl.ds(8, 8), :], dst.at[pl.ds(p, 4), :, pl.ds(0, 8), :])
                else:
                    copy(b.at[:, :, pl.ds(half, 32), :], dst.at[pl.ds(p, 4), :, pl.ds(OWN - 8, 32), :])
            copy(group[8].at[f, :, pl.ds(half, 32), :], dst.at[(PLANES - 1) * side, :, pl.ds(OWN - 8, 32), :])
    for c in copies:
        c.wait()

    lane = lax.broadcasted_iota(jnp.int32, (8, LANES), 1)
    row = lax.broadcasted_iota(jnp.int32, (8, LANES), 0)
    first, last = lane == 0, lane == LANES - 1

    def take_segments(p, _):
        for h in range(2):
            segs[h, pl.ds(p, 1), :] = q[p, h, pl.ds(16 * (1 - core), 1), :]
        return 0

    lax.fori_loop(0, PLANES, take_segments, 0)
    here = [jnp.where(at_edge & (core == c), 1.0, 0.0) for c in range(2)]
    for h in range(2):
        s = segs[h]
        acc = [jnp.zeros_like(s) for _ in range(SLICES)]
        for m in range(SEGMENTS):
            hit = s == jnp.float32(m)
            for n in range(SLICES):
                change = controls[n, m] - controls[n - 1, m] if n > 0 else controls[n, m]
                acc[n] = jnp.where(hit, change, acc[n])
        for n in range(SLICES):
            jumps[0, n, h] = acc[n] * here[0]
            if n < 3:
                jumps[1, n, h] = acc[n] * here[1] if n < 2 else jnp.zeros_like(s)

    def step(*stages):
        blocks, room = [], 0
        for stage, part in stages:
            part = list(part)
            while part:
                if room < 8:
                    blocks.append([])
                    room = MOST
                blocks[-1].append((stage, part[:room]))
                part, room = part[room:], room - min(room, len(part))
        for block in blocks:
            def body(_, carry, block=block):
                stores = []
                for stage, part in block:
                    stage(stores, part)
                for ref, p, h, y, value in stores:
                    ref[p, h, pl.ds(y, 8), :] = value
                return carry

            lax.fori_loop(0, trips, body, 0)

    def loader():
        cache = {}

        def load(ref, p, h, y, base=0):
            key = (id(ref), p, h, y)
            if key not in cache:
                cache[key] = ref[base + p, h, pl.ds(zero + y, 8), :]
            return cache[key]

        return load

    def around(ref, load, p, y, base=0):
        even, odd = load(ref, p, 0, y, base), load(ref, p, 1, y, base)
        z = (odd + jnp.where(first, 0.0, pltpu.roll(odd, 1, 1)), even + jnp.where(last, 0.0, pltpu.roll(even, LANES - 1, 1)))
        return [z[h] + (load(ref, p, h, y - 1, base) + load(ref, p, h, y + 1, base))
                + (load(ref, p - 1, h, y, base) + load(ref, p + 1, h, y, base)) for h in range(2)]

    def cells(r):
        for y, planes in tiles(r):
            for p in planes:
                yield y, p

    def jump(n, p, h, y, both):
        result = None
        for which, at in ((0, OWN), (1, OWN - 16)):
            if y <= at < y + 8 and (which == 0 or both):
                value = jnp.where(row == at - y, jumps[which, n, h, pl.ds(p, 1), :], 0.0)
                result = value if result is None else result + value
        return result

    def setup(stores, part):
        load = loader()
        for y, p in part:
            for h in range(2):
                c = load(sig, p, h, y)
                inside = c > 0.0
                c = jnp.where(inside, c, 1.0)
                s = jnp.where(inside, COARSE / c, 0.0)
                d = jnp.where(inside, 1.0 / (c + 6.0), 0.0)
                value = load(q, p, h, y)
                change = jump(0, p, h, y, True)
                if change is not None:
                    value = value + change
                    stores.append((q, p, h, zero + y, value))
                stores += [(sig, p, h, zero + y, s), (rd, p, h, zero + y, d), (v, p, h, zero + y, s * value),
                           (wa, p, h, zero + y, d * value)]

    def clear(stores, part):
        nothing = jnp.zeros((8, LANES), jnp.float32)
        for p in range(REACH - 7, REACH + 11):
            for h in range(2):
                for y in range(OWN - 16, OWN + 32, 8):
                    stores.append((hh, p, h, y, nothing))
        for p in range(4):
            for h in range(2):
                stores += [(total, p, h, 0, nothing), (total, p, h, 8, nothing)]

    def advance(n, r, old, new, both):
        def stage(stores, part):
            load = loader()
            for y, p in part:
                sums = around(v, load, p, y, old)
                for h in range(2):
                    value = load(q, p, h, y) + (sums[h] - 6.0 * load(v, p, h, y))
                    change = jump(n, p, h, y, both)
                    if change is not None:
                        value = value + change
                    stores.append((q, p, h, zero + y, value))
                    if new is not None:
                        stores += [(v, new + p, h, zero + y, load(sig, p, h, y) * value),
                                   (wa, p, h, zero + y, load(rd, p, h, y) * value)]
        return stage, cells(r)

    def second_order(r):
        def stage(stores, part):
            load = loader()
            for y, p in part:
                sums = around(e, load, p, y)
                for h in range(2):
                    value = sums[h] - 6.0 * load(e, p, h, y)
                    stores += [(le, p, h, zero + y, value), (ua, p, h, zero + y, load(rd, p, h, y) * value)]
        return stage, cells(r)

    def with_source(stores, part):
        load = loader()
        for y, p in part:
            for h in range(2):
                value = load(le, p, h, y) + load(q, p, h, y)
                stores += [(le, p, h, zero + y, value), (ua, p, h, zero + y, load(rd, p, h, y) * value)]

    def sweep(r, src, dst, source):
        def stage(stores, part):
            load = loader()
            for y, p in part:
                sums = around(src, load, p, y)
                for h in range(2):
                    stores.append((dst, p, h, zero + y, load(rd, p, h, y) * (load(source, p, h, y) + sums[h])))
        return stage, cells(r)

    def finish_first(initial, r, src):
        def stage(stores, part):
            load = loader()
            for y, p in part:
                sums = around(src, load, p, y)
                for h in range(2):
                    value = load(rd, p, h, y) * (load(q, p, h, y) + sums[h])
                    s = load(sig, p, h, y)
                    if initial:
                        value = value - s * load(q, p, h, y)
                    else:
                        value = load(e, p, h, y) + (value + s * (load(le, p, h, y) - load(q, p, h, y)))
                    stores.append((e, p, h, zero + y, value))
        return stage, cells(r)

    def finish_second(r, src, old, new):
        def stage(stores, part):
            load = loader()
            for y, p in part:
                sums = around(src, load, p, y)
                around_h = around(hh, load, p, y, old)
                for h in range(2):
                    value = load(rd, p, h, y) * (load(le, p, h, y) + sums[h])
                    coarse = around_h[h] - 6.0 * load(hh, p, h, y)
                    if new is not None:
                        coarse = coarse - load(le, p, h, y)
                    value = load(hh, p, h, y) + (value + load(sig, p, h, y) * coarse)
                    if new is not None:
                        stores.append((hh, new + p, h, zero + y, value))
                    else:
                        value = value + total[p - REACH, h, pl.ds(y - OWN, 8), :] + load(e, p, h, y)
                        stores.append((ends, (SLICES - 1) * 4 + p - REACH, h, y - OWN, value))
        return stage, cells(r)

    def close(n, old):
        def stage(stores, part):
            for y, p in part:
                for h in range(2):
                    value = v[old + p, h, pl.ds(y, 8), :] + total[p - REACH, h, pl.ds(y - OWN, 8), :]
                    stores.append((total, p - REACH, h, y - OWN, value))
                    value = value + e[p, h, pl.ds(y, 8), :] + hh[old + p, h, pl.ds(y, 8), :]
                    stores.append((ends, (n - 1) * 4 + p - REACH, h, y - OWN, value))
        return stage, cells(0)

    def sweeps(n, r_w, r_u, old, new, initial=False):
        w, u = (wa, wb), (ua, ub)
        for k in range(SWEEPS - 1):
            stages = []
            if r_w is not None:
                stages.append(sweep(r_w - k, *w, q) if k < SWEEPS - 2 else finish_first(initial, r_w - k, w[0]))
            if r_u is not None:
                stages.append(sweep(r_u - k, *u, le) if k < SWEEPS - 2 else finish_second(r_u - k, u[0], old, new))
            step(*stages)
            w, u = w[::-1], u[::-1]

    step((setup, cells(17)), (clear, [None]))
    sweeps(0, 16, None, None, None, True)
    for start in range(1, SLICES - 1, 2):
        def slice_pair(j, carry, start=start):
            n = start + j
            old, new = PLANES * j, PLANES * (1 - j)
            step(close(n, old), second_order(12 - start), advance(n, 17 - start, old, new, start == 1))
            sweeps(n, 16 - start, 11 - start, old, new)
            return carry

        lax.fori_loop(0, 2, slice_pair, 0)
    step(close(SLICES - 1, 0), second_order(5), advance(SLICES - 1, 5, 0, None, False))
    step((with_source, cells(5)))
    sweeps(SLICES - 1, None, 4, 0, None)

    both = jnp.concatenate([ends[:, h].reshape(SLICES * 4 * 16, LANES) for h in range(2)], axis=1)
    whole = lax.dot_general(both, order[...], (((1,), (1,)), ((), ())), precision=lax.Precision.HIGHEST,
                            preferred_element_type=jnp.float32)
    out[...] = whole.reshape(SLICES, 4, 16, 256)


def solve(controls, *blocks):
    field = pltpu.VMEM((PLANES, 2, ROWS, LANES), jnp.float32)
    two = pltpu.VMEM((2 * PLANES, 2, ROWS, LANES), jnp.float32)
    any_space = pl.BlockSpec(memory_space=pl.ANY)
    smem = pl.BlockSpec(memory_space=pltpu.SMEM)
    vmem = pl.BlockSpec(memory_space=pltpu.VMEM)
    return pl.pallas_call(
        main_kernel,
        out_shape=jax.ShapeDtypeStruct((SLICES, 4, 16, 256), jnp.float32),
        in_specs=[smem] + [any_space] * len(blocks) + [vmem],
        out_specs=vmem,
        scratch_shapes=[field] * 3 + [two] + [field] * 6 + [two] + [
            pltpu.VMEM((4, 2, 16, LANES), jnp.float32),
            pltpu.VMEM((2, SLICES, 2, 40, LANES), jnp.float32),
            pltpu.VMEM((2, 40, LANES), jnp.float32),
            pltpu.VMEM((SLICES * 4, 2, 16, LANES), jnp.float32),
            pltpu.SemaphoreType.DMA((24,)),
        ],
        compiler_params=pltpu.CompilerParams(vmem_limit_bytes=60 << 20),
        name="parareal",
    )(controls, *blocks, jnp.asarray(lane_order()))


def on_device(initial_state, capacity, source, control, segment_index):
    tm, chip, core = lax.axis_index("tm"), lax.axis_index("chip"), lax.axis_index("core")
    block = jnp.where(chip >= CHIPS // 2, tm ^ 4, tm)
    rows = lax.broadcasted_iota(jnp.int32, (SLICES, 1), 0)
    controls = jnp.where(rows == tm, control, 0.0)

    def spread(controls, bit):
        return controls + lax.ppermute(controls, "tm", [(t, t ^ bit) for t in range(SLICES)])

    first = spread(controls, 1)

    above = jnp.zeros((2, 25, 256), jnp.float32)
    marked = above.at[:, 17, :].set(segment_index.astype(jnp.float32))

    def window(x, top):
        return lax.dynamic_slice_in_dim(jnp.concatenate([top, x, above], axis=1), 32 * block, 82, axis=1)

    def beside(x):
        y = send(x, PARTNER)
        return jnp.where(core == 0, jnp.concatenate([x, y], axis=-3), jnp.concatenate([y, x], axis=-3))

    chip_c = beside(window(capacity, above))
    mine = jnp.stack([window(source, marked), window(initial_state, above)])
    outer = jnp.where(core == 0, mine[1, 0], mine[1, 1])
    facing = send(outer, FACING)
    facing_same = send(outer, FACING_SAME)
    chip4 = beside(mine)
    before = jnp.where(core == 0, facing, facing_same)
    after = jnp.where(core == 0, facing_same, facing)
    state = jnp.concatenate([before[None], chip4[1], after[None]], axis=0)
    middle = state[1:-1, 1:-1]
    deeper = jnp.pad(middle, ((0, 0), (0, 0), (1, 1)))
    residual = (state[2:, 1:-1] + state[:-2, 1:-1] + state[1:-1, 2:] + state[1:-1, :-2]
                + deeper[:, :, 2:] + deeper[:, :, :-2] - 6.0 * middle + chip4[0, :, 1:-1])
    order = jnp.asarray(lane_order())

    def laid(x):
        return jnp.stack([jnp.dot(x, order[:, h * LANES:(h + 1) * LANES], precision=lax.Precision.HIGHEST)
                          for h in range(2)], axis=1)

    own_c, own_q = laid(chip_c[:, 1:-1]), laid(residual)
    x_c, x_q = own_c[:, :, 8:72], own_q[:, :, 8:72]
    got = []
    edge = jnp.stack([own_c, own_q])[:, :, :, 16:64]
    edge = jnp.where(core == 0, edge[:, 3], edge[:, 0])
    for k in range(4):
        if k == 2:
            x_c, x_q = x_c[:, :, 8:56], x_q[:, :, 8:56]
        x_c, x_q = send(x_c, OUTWARD), send(x_q, OUTWARD)
        got += [x_c, x_q]
        if k == 0:
            first, x_c = lax.optimization_barrier((first, x_c))
            second = spread(first, 2)
        if k == 1:
            edge, second, x_c = lax.optimization_barrier((edge, second, x_c))
            end_cq = send(edge, OUTWARD_5)
            controls = spread(second, 4)
    got.append(end_cq)
    passed = [send(x, PARTNER) for x in got]
    ends = solve(controls, own_c, own_q, *got, *passed)

    split = ends.reshape(SLICES * 2, 2, 16, 256)
    mixed = lax.all_to_all(split, ("tm", "core"), split_axis=0, concat_axis=0, tiled=True).reshape(2, 4, 2, 2, 16, 256)
    mixed = jnp.where(chip >= CHIPS // 2, mixed[::-1], mixed)
    whole = mixed.transpose(3, 0, 1, 2, 4, 5).reshape(2, 256, 256)
    return (whole + initial_state)[None]


def solution(mesh):
    split = Mesh(mesh.devices.reshape(8, CHIPS, 2), AXES)
    space = ("chip", "core")
    in_specs = (P(space, None, None), P(space, None, None), P(space, None, None), P("tm", None), P(space, None))
    return jax.shard_map(on_device, mesh=split, in_specs=in_specs, out_specs=P("tm", space, None, None), check_vma=False)
```
